32 devices in a mesh: query: 8 (over y, x, core), tok: 4 (over z).
Axes of the slice: x: 2, y: 2, z: 4, core: 2. Of those that a mesh axis runs over, the one named last changes fastest.
Arguments:
- query_acts: bfloat16 [8, 1024, 4096], P('query', 'tok'), may hold values from -6 to 6
- query_grads: bfloat16 [8, 1024, 512], P('query', 'tok'), may hold values from -6 to 6
- sketch_maps: bfloat16 [8, 32, 512], P('query'), may hold values from -0.25 to 0.25
- res_acts: bfloat16 [32768, 4096], P(('query', 'tok')), may hold values from -6 to 6
- res_grads: bfloat16 [32768, 512], P(('query', 'tok')), may hold values from -6 to 6
Outputs:
- scores: float32 [8, 32768], P(None, ('query', 'tok'))
The draws below stay inside these ranges and needn't reach their ends.
All inputs are finite; a program needn't handle non-finite values.
Results may differ from the reference program's by a relative error of at most 0.0054.
Values may be sent and summed in bfloat16 or wider, within the bound.
A program may use at most 64 MiB of HBM per device.

```python
import math
import jax
import jax.numpy as jnp
from jax import lax

DIN = 4096
DOUT = 512
RANK = 32
RES_DEV = 1024
NQ = 8
QTOK = 1024
RTOK = 32768


def block_levels(own_key, shape, cuts, smallest, high):
    gain, own = 1.0, jax.random.fold_in(own_key, 6)
    for axis_at, blocks in cuts:
        draws = jnp.exp(jax.random.uniform(jax.random.fold_in(own, axis_at), (blocks,), jnp.float32, smallest / len(cuts), high / len(cuts)))
        gain = gain * jnp.repeat(draws, shape[axis_at] // blocks).reshape([-1 if axis == axis_at else 1 for axis in range(len(shape))])
    return gain


def normal_values(stream_key, shape, scale, reach, split=(), kind=jnp.bfloat16):
    gain = block_levels(stream_key, shape, split, -0.22, 0.18) if split else 1.0
    entries = jax.random.normal(stream_key, shape, jnp.float32) * scale * gain
    return jnp.minimum(jnp.maximum(entries, -reach), reach).astype(kind)


def setup_inputs(seed: int = 0) -> dict:
    key_list = jax.random.split(jax.random.key(seed), 6)
    query_acts = normal_values(key_list[0], (NQ, QTOK, DIN), 1.0, 6.0, ((0, 8), (1, 4)))
    query_grads = normal_values(key_list[1], (NQ, QTOK, DOUT), 1.0, 6.0, ((0, 8), (1, 4)))
    sketch_maps = normal_values(key_list[2], (NQ, RANK, DOUT), DOUT ** -0.5, 0.25, ((0, 8),))
    res_acts = normal_values(key_list[3], (RTOK, DIN), 1.0, 6.0, ((0, 32),))
    res_grads = normal_values(key_list[4], (RTOK, DOUT), 1.0, 6.0, ((0, 32),))
    return {"query_acts": query_acts, "query_grads": query_grads, "sketch_maps": sketch_maps, "res_acts": res_acts, "res_grads": res_grads}


def factors(query_act, query_grad, sketch_map):
    projected = lax.dot_general(sketch_map.astype(jnp.float32), query_grad.astype(jnp.float32), (((1,), (1,)), ((), ())), preferred_element_type=jnp.float32).astype(jnp.bfloat16)
    sketch = jnp.dot(projected.astype(jnp.float32), query_act.astype(jnp.float32), preferred_element_type=jnp.float32)
    gram_matrix = jnp.dot(sketch, sketch.T, precision=lax.Precision.HIGHEST)
    lower_factor = jnp.linalg.cholesky(gram_matrix)
    left_factor = lax.linalg.triangular_solve(lower_factor, sketch, left_side=True, lower=True).astype(jnp.bfloat16)
    pulled = lax.dot_general(left_factor.astype(jnp.float32), query_act.astype(jnp.float32), (((1,), (1,)), ((), ())), preferred_element_type=jnp.float32).astype(jnp.bfloat16)
    right_factor = jnp.dot(pulled.astype(jnp.float32), query_grad.astype(jnp.float32), preferred_element_type=jnp.float32).astype(jnp.bfloat16)
    return (left_factor, right_factor)

def reference(query_acts, query_grads, sketch_maps, res_acts, res_grads):
    left_all, right_all = lax.map(lambda items: factors(items[0], items[1], items[2]), (query_acts, query_grads, sketch_maps))
    left_all = left_all.reshape(NQ * RANK, DIN)
    right_all = right_all.reshape(NQ * RANK, DOUT)
    score_scale = 1.0 / math.sqrt(RANK * DOUT * QTOK)
    block_count = RTOK // RES_DEV
    act_blocks = res_acts.reshape(block_count, RES_DEV, DIN)
    grad_blocks = res_grads.reshape(block_count, RES_DEV, DOUT)

    def one_block(items):
        on_left = lax.dot_general(left_all.astype(jnp.float32), items[0].astype(jnp.float32), (((1,), (1,)), ((), ())), preferred_element_type=jnp.float32)
        on_right = lax.dot_general(right_all.astype(jnp.float32), items[1].astype(jnp.float32), (((1,), (1,)), ((), ())), preferred_element_type=jnp.float32)
        product = (on_left * on_right).reshape(NQ, RANK, RES_DEV)
        return lax.optimization_barrier(jnp.sum(product, axis=1)) * score_scale
    blocks = lax.map(one_block, (act_blocks, grad_blocks))
    return jnp.transpose(blocks, (1, 0, 2)).reshape(NQ, RTOK)
```

```python
import functools
import math

import jax
import jax.numpy as jnp
from jax import lax
from jax.experimental import pallas as pl
from jax.experimental.pallas import tpu as pltpu
from jax.sharding import PartitionSpec as P

MESH = pl.DeviceIdType.MESH
F32 = jnp.float32
BF16 = jnp.bfloat16


def contract_last(first_arr, second_arr):
    return lax.dot_general(first_arr, second_arr, (((1,), (1,)), ((), ())), preferred_element_type=F32)


def spd_inverse(gram):
    size = gram.shape[0]
    rows = lax.broadcasted_iota(jnp.int32, (size, 2 * size), 0)
    cols = lax.broadcasted_iota(jnp.int32, (size, size), 1)
    eye = jnp.where(rows[:, :size] == cols, 1.0, 0.0).astype(F32)
    aug = jnp.concatenate([gram, eye], axis=1)
    for k in range(size):
        row = aug[k : k + 1, :] / aug[k : k + 1, k : k + 1]
        aug = jnp.where(rows == k, row, aug - aug[:, k : k + 1] * row)
    return aug[:, size:]


def kernel(
    n_q, n_t, scale,
    a_hbm, g_hbm, m_hbm, ra_hbm, rg_hbm, out_ref,
    a_buf, g_buf, m_buf, ra_buf, rg_buf,
    part_buf, rs_buf, s_all, r_mine, r_recv, x_all, acc,
    local_sem, rs_s, rs_r, z_s, z_r, c_s, c_r, b_s, b_r, f_s, f_r, x_s, x_r,
):
    q, z = lax.axis_index("query"), lax.axis_index("tok")
    n_chip = n_q // 2
    chip, core = q // 2, lax.rem(q, 2)
    sibling = chip * 2 + 1 - core
    rank = m_buf.shape[0]
    width = a_buf.shape[2]

    def tok_at(i):
        return lax.rem(z + i + n_t, n_t)

    def chip_at(c, which):
        return lax.rem(chip + c + n_chip, n_chip) * 2 + which

    loads = []

    def load(src, dst):
        copy = pltpu.make_async_copy(src, dst, local_sem.at[len(loads)])
        copy.start()
        loads.append(copy)
        return copy

    load_m = load(m_hbm, m_buf)
    load_g = load(g_hbm, g_buf)
    load_a, load_ra = [], []
    for i in range(n_t):
        t = tok_at(i + 1)
        load_a.append(load(a_hbm.at[:, pl.ds(pl.multiple_of(t * width, width), width)], a_buf.at[t]))
    barrier = pltpu.get_barrier_semaphore()
    for i in range(1, n_t):
        pl.semaphore_signal(barrier, inc=1, device_id=(q, tok_at(i)), device_id_type=MESH)
    for i in range(1, n_q):
        pl.semaphore_signal(barrier, inc=1, device_id=(lax.rem(q + i, n_q), z), device_id_type=MESH)

    sent = []

    def send(src, dst, send_sem, recv_sem, device):
        copy = pltpu.make_async_remote_copy(
            src_ref=src, dst_ref=dst, send_sem=send_sem, recv_sem=recv_sem, device_id=device, device_id_type=MESH
        )
        copy.start()
        sent.append(copy)

    def landed(dst, send_sem, recv_sem, device):
        pltpu.make_async_remote_copy(
            src_ref=dst, dst_ref=dst, send_sem=send_sem, recv_sem=recv_sem, device_id=device, device_id_type=MESH
        ).wait_recv()

    load_m.wait()
    load_g.wait()
    projected = contract_last(m_buf[...], g_buf[...]).astype(BF16)
    chunk = None
    for i in range(1, n_t + 1):
        t = tok_at(i)
        load_a[i - 1].wait()
        part = jnp.dot(projected, a_buf[t], preferred_element_type=F32)
        if i == n_t:
            chunk = part
        else:
            part_buf[i - 1] = part.astype(BF16)
    for i in range(n_t):
        t = tok_at(-i)
        load_ra.append(load(ra_hbm.at[:, pl.ds(pl.multiple_of(t * width, width), width)], ra_buf.at[t]))
    load_rg = load(rg_hbm, rg_buf)
    pl.semaphore_wait(barrier, n_t - 1 + n_q - 1)
    for i in range(1, n_t):
        send(part_buf.at[i - 1], rs_buf.at[i - 1], rs_s.at[i - 1], rs_r.at[i - 1], (q, tok_at(i)))
    for i in range(1, n_t):
        landed(rs_buf.at[i - 1], rs_s.at[i - 1], rs_r.at[i - 1], (q, tok_at(-i)))
        chunk = chunk + rs_buf[i - 1].astype(F32)

    def block(t, owner):
        return s_all.at[t, pl.ds(pl.multiple_of(owner * rank, rank), rank), :]

    s_all[z, pl.ds(pl.multiple_of(q * rank, rank), rank), :] = chunk.astype(BF16)

    def spread(i):
        here = block(tok_at(-i), q)
        for c in range(1, n_chip):
            send(here, here, c_s.at[c - 1, i], c_r.at[c - 1, i], (chip_at(c, core), z))
        send(here, here, b_s.at[0, i], b_r.at[0, i], (sibling, z))

    for i in range(1, n_t):
        send(block(z, q), block(z, q), z_s.at[i - 1], z_r.at[i - 1], (q, tok_at(i)))
    gram = jnp.zeros((rank, rank), F32)
    pulled = jnp.zeros((rank, g_buf.shape[0]), F32)
    for i in range(n_t):
        t = tok_at(-i)
        if i:
            landed(block(t, q), z_s.at[i - 1], z_r.at[i - 1], (q, t))
        spread(i)
        mine = s_all[t, pl.ds(pl.multiple_of(q * rank, rank), rank), :]
        pulled += contract_last(mine, a_buf[t])
        gram += contract_last(mine, mine)
    high = pulled.astype(BF16)
    low = (pulled - high.astype(F32)).astype(BF16)
    grads = g_buf[...]
    right = jnp.dot(high, grads, preferred_element_type=F32) + jnp.dot(low, grads, preferred_element_type=F32)
    r_mine[...] = right.astype(BF16)
    for i in range(1, n_t):
        send(r_mine, r_recv.at[i - 1], f_s.at[i - 1], f_r.at[i - 1], (q, tok_at(i)))

    def relay(i):
        t = tok_at(-i)
        for c in range(1, n_chip):
            owner = chip_at(-c, core)
            landed(block(t, owner), c_s.at[c - 1, i], c_r.at[c - 1, i], (owner, z))
            send(block(t, owner), block(t, owner), b_s.at[c, i], b_r.at[c, i], (sibling, z))

    def score(i):
        t = tok_at(-i)
        for c in range(n_chip):
            landed(block(t, chip_at(-c, 1 - core)), b_s.at[c, i], b_r.at[c, i], (sibling, z))
        load_ra[i].wait()
        term = contract_last(s_all[t], ra_buf[t])
        if i == 0:
            acc[...] = term
        else:
            acc[...] += term


    def x_block(owner):
        return x_all.at[pl.ds(pl.multiple_of(owner * rank, rank), rank), :]

    def solve(inverse, right):
        for i in range(1, n_t):
            landed(r_recv.at[i - 1], f_s.at[i - 1], f_r.at[i - 1], (q, tok_at(-i)))
            right = right + r_recv[i - 1].astype(F32)
        solved = jnp.dot(inverse, right, precision=lax.Precision.HIGHEST, preferred_element_type=F32)
        x_all[pl.ds(pl.multiple_of(q * rank, rank), rank), :] = solved.astype(BF16)
        for i in (*range(2, n_q), 1):
            send(x_block(q), x_block(q), x_s.at[i - 1], x_r.at[i - 1], (lax.rem(q + i, n_q), z))

    relay(0)
    inverse = spd_inverse(gram)
    relay(1)
    solve(inverse, right)
    score(0)
    for i in range(2, n_t):
        relay(i)
        score(i - 1)
    score(n_t - 1)
    load_rg.wait()
    for i in range(1, n_q):
        owner = lax.rem(q + n_q - i, n_q)
        landed(x_block(owner), x_s.at[i - 1], x_r.at[i - 1], (owner, z))
    product = contract_last(x_all[...], rg_buf[...]) * acc[...]
    totals = jnp.sum(product.reshape(n_q, rank, product.shape[1]), axis=1)
    out_ref[...] = totals * scale
    for copy in sent:
        copy.wait_send()


def local(query_acts, query_grads, sketch_maps, res_acts, res_grads):
    n_q, n_t = lax.axis_size("query"), lax.axis_size("tok")
    _, tokens, d_in = query_acts.shape
    d_out = query_grads.shape[2]
    rank = sketch_maps.shape[1]
    resident = res_acts.shape[0]
    width = d_in // n_t
    scale = 1.0 / math.sqrt(rank * d_out * tokens * n_t)
    n_chip = n_q // 2
    dma = pltpu.SemaphoreType.DMA
    vmem = pltpu.VMEM
    any_spec = pl.BlockSpec(memory_space=pl.ANY)
    return pl.pallas_call(
        functools.partial(kernel, n_q, n_t, scale),
        out_shape=pltpu.VMEM((n_q, resident), F32),
        in_specs=[any_spec] * 5,
        out_specs=pl.BlockSpec(memory_space=pltpu.VMEM),
        scratch_shapes=[
            vmem((n_t, tokens, width), BF16),
            vmem((tokens, d_out), BF16),
            vmem((rank, d_out), BF16),
            vmem((n_t, resident, width), BF16),
            vmem((resident, d_out), BF16),
            vmem((n_t - 1, rank, width), BF16),
            vmem((n_t - 1, rank, width), BF16),
            vmem((n_t, n_q * rank, width), BF16),
            vmem((rank, d_out), BF16),
            vmem((n_t - 1, rank, d_out), BF16),
            vmem((n_q * rank, d_out), BF16),
            vmem((n_q * rank, resident), F32),
            dma((2 * n_t + 3,)),
            dma((n_t - 1,)), dma((n_t - 1,)),
            dma((n_t - 1,)), dma((n_t - 1,)),
            dma((n_chip - 1, n_t)), dma((n_chip - 1, n_t)),
            dma((n_chip, n_t)), dma((n_chip, n_t)),
            dma((n_t - 1,)), dma((n_t - 1,)),
            dma((n_q - 1,)), dma((n_q - 1,)),
        ],
        compiler_params=pltpu.CompilerParams(
            collective_id=0, has_side_effects=True, vmem_limit_bytes=60 * 1024 * 1024
        ),
    )(query_acts[0], query_grads[0], sketch_maps[0], res_acts, res_grads)


def solution(mesh):
    in_specs = (
        P("query", "tok", None),
        P("query", "tok", None),
        P("query", None, None),
        P(("query", "tok"), None),
        P(("query", "tok"), None),
    )
    out_specs = P(None, ("query", "tok"))
    return jax.shard_map(local, mesh=mesh, in_specs=in_specs, out_specs=out_specs, check_vma=False)
```

```python
import functools
import math

import jax
import jax.numpy as jnp
from jax import lax
from jax.experimental import pallas as pl
from jax.experimental.pallas import tpu as pltpu
from jax.sharding import PartitionSpec as P

MESH = pl.DeviceIdType.MESH
F32 = jnp.float32
BF16 = jnp.bfloat16


def contract_last(first_arr, second_arr):
    return lax.dot_general(first_arr, second_arr, (((1,), (1,)), ((), ())), preferred_element_type=F32)


def spd_inverse(gram):
    size = gram.shape[0]
    rows = lax.broadcasted_iota(jnp.int32, (size, 2 * size), 0)
    cols = lax.broadcasted_iota(jnp.int32, (size, size), 1)
    eye = jnp.where(rows[:, :size] == cols, 1.0, 0.0).astype(F32)
    aug = jnp.concatenate([gram, eye], axis=1)
    for k in range(size):
        row = aug[k : k + 1, :] / aug[k : k + 1, k : k + 1]
        aug = jnp.where(rows == k, row, aug - aug[:, k : k + 1] * row)
    return aug[:, size:]


def kernel(
    n_q, n_t, scale,
    a_hbm, g_hbm, m_hbm, ra_hbm, rg_hbm, out_ref,
    a_buf, g_buf, m_buf, ra_buf, rg_buf,
    part_buf, rs_buf, s_all, r_mine, r_recv, x_all, acc,
    local_sem, rs_s, rs_r, z_s, z_r, s_s, c_r, b_r, f_s, f_r, x_s, x_r,
):
    q, z = lax.axis_index("query"), lax.axis_index("tok")
    n_chip = n_q // 2
    chip, core = q // 2, lax.rem(q, 2)
    sibling = chip * 2 + 1 - core
    rank = m_buf.shape[0]
    width = a_buf.shape[2]

    def tok_at(i):
        return lax.rem(z + i + n_t, n_t)

    def chip_at(c, which):
        return lax.rem(chip + c + n_chip, n_chip) * 2 + which

    def load(src, dst, sem):
        copy = pltpu.make_async_copy(src, dst, local_sem.at[sem])
        copy.start()
        return copy

    load_m = load(m_hbm, m_buf, 0)
    load_g = load(g_hbm, g_buf, 1)
    load_a, load_ra = [], []
    for i in range(n_t):
        t = tok_at(i + 1)
        load_a.append(load(a_hbm.at[:, pl.ds(pl.multiple_of(t * width, width), width)], a_buf.at[t], 2 + i))
    barrier = pltpu.get_barrier_semaphore()
    for i in range(1, n_t):
        pl.semaphore_signal(barrier, inc=1, device_id=(q, tok_at(i)), device_id_type=MESH)
    for i in range(1, n_q):
        pl.semaphore_signal(barrier, inc=1, device_id=(lax.rem(q + i, n_q), z), device_id_type=MESH)

    def remote(src, dst, send_sem, recv_sem, device):
        return pltpu.make_async_remote_copy(
            src_ref=src, dst_ref=dst, send_sem=send_sem, recv_sem=recv_sem, device_id=device, device_id_type=MESH
        )

    def send(src, dst, send_sem, recv_sem, device):
        remote(src, dst, send_sem, recv_sem, device).start()

    def landed(like, sem):
        remote(like, like, sem, sem, (sibling, z)).wait_recv()

    def left(like, sem):
        remote(like, like, sem, sem, (sibling, z)).wait_send()

    load_m.wait()
    load_g.wait()
    projected = contract_last(m_buf[...], g_buf[...]).astype(BF16)
    chunk = None
    for i in range(1, n_t + 1):
        t = tok_at(i)
        load_a[i - 1].wait()
        part = jnp.dot(projected, a_buf[t], preferred_element_type=F32)
        if i == n_t:
            chunk = part
        else:
            part_buf[i - 1] = part.astype(BF16)
    for i in range(n_t):
        t = tok_at(-i)
        load_ra.append(load(ra_hbm.at[:, pl.ds(pl.multiple_of(t * width, width), width)], ra_buf.at[t], 2 + i))
    load_rg = load(rg_hbm, rg_buf, 0)
    pl.semaphore_wait(barrier, n_t - 1 + n_q - 1)
    for i in range(1, n_t):
        send(part_buf.at[i - 1], rs_buf.at[i - 1], rs_s, rs_r.at[i - 1], (q, tok_at(i)))
    for i in range(1, n_t):
        landed(rs_buf.at[i - 1], rs_r.at[i - 1])
        chunk = chunk + rs_buf[i - 1].astype(F32)

    def block(t, owner):
        return s_all.at[t, pl.ds(pl.multiple_of(owner * rank, rank), rank), :]

    s_all[z, pl.ds(pl.multiple_of(q * rank, rank), rank), :] = chunk.astype(BF16)

    def from_chip(c, i):
        return c_r.at[c - 1, i]

    def spread(i):
        here = block(tok_at(-i), q)
        for c in range(1, n_chip):
            send(here, here, s_s, from_chip(c, i), (chip_at(c, core), z))
        send(here, here, s_s, b_r.at[i], (sibling, z))

    for i in range(1, n_t):
        send(block(z, q), block(z, q), z_s, z_r.at[i - 1], (q, tok_at(i)))
    gram = jnp.zeros((rank, rank), F32)
    pulled = jnp.zeros((rank, g_buf.shape[0]), F32)
    for i in range(n_t):
        t = tok_at(-i)
        if i:
            landed(block(t, q), z_r.at[i - 1])
        spread(i)
        mine = s_all[t, pl.ds(pl.multiple_of(q * rank, rank), rank), :]
        pulled += contract_last(mine, a_buf[t])
        if i < n_t - 1:
            gram += contract_last(mine, mine)
    high = pulled.astype(BF16)
    low = (pulled - high.astype(F32)).astype(BF16)
    grads = g_buf[...]
    right = jnp.dot(high, grads, preferred_element_type=F32) + jnp.dot(low, grads, preferred_element_type=F32)
    r_mine[...] = right.astype(BF16)
    for i in range(1, n_t):
        send(r_mine, r_recv.at[i - 1], f_s, f_r, (q, tok_at(i)))
    gram += contract_last(mine, mine)

    def relay(i):
        t = tok_at(-i)
        for c in range(1, n_chip):
            here = block(t, chip_at(-c, core))
            landed(here, from_chip(c, i))
            send(here, here, s_s, b_r.at[i], (sibling, z))

    def ready(i):
        landed(s_all.at[tok_at(-i), pl.ds(0, n_chip * rank)], b_r.at[i])
        load_ra[i].wait()

    def term(i):
        t = tok_at(-i)
        return contract_last(s_all[t], ra_buf[t])

    def score(i):
        ready(i)
        if i == 0:
            acc[...] = term(i)
        else:
            acc[...] += term(i)

    def x_block(owner):
        return x_all.at[pl.ds(pl.multiple_of(owner * rank, rank), rank), :]

    def solve(inverse, right):
        landed(r_recv, f_r)
        for i in range(1, n_t):
            right = right + r_recv[i - 1].astype(F32)
        solved = jnp.dot(inverse, right, precision=lax.Precision.HIGHEST, preferred_element_type=F32)
        x_all[pl.ds(pl.multiple_of(q * rank, rank), rank), :] = solved.astype(BF16)
        for i in (*range(2, n_q), 1):
            send(x_block(q), x_block(q), x_s, x_r, (lax.rem(q + i, n_q), z))

    relay(0)
    inverse = spd_inverse(gram)
    relay(1)
    solve(inverse, right)
    score(0)
    for i in range(2, n_t):
        relay(i)
        score(i - 1)
    ready(n_t - 1)
    load_rg.wait()
    others = x_all.at[pl.ds(0, (n_q - 1) * rank), :]
    landed(others, x_r)
    product = contract_last(x_all[...], rg_buf[...]) * (acc[...] + term(n_t - 1))
    totals = jnp.sum(product.reshape(n_q, rank, product.shape[1]), axis=1)
    out_ref[...] = totals * scale
    left(part_buf, rs_s)
    left(rs_buf, z_s)
    left(s_all.at[:, pl.ds(0, (n_q - 1) * rank), :], s_s)
    left(r_recv, f_s)
    left(others, x_s)


def local(query_acts, query_grads, sketch_maps, res_acts, res_grads):
    n_q, n_t = lax.axis_size("query"), lax.axis_size("tok")
    _, tokens, d_in = query_acts.shape
    d_out = query_grads.shape[2]
    rank = sketch_maps.shape[1]
    resident = res_acts.shape[0]
    width = d_in // n_t
    scale = 1.0 / math.sqrt(rank * d_out * tokens * n_t)
    n_chip = n_q // 2
    dma = pltpu.SemaphoreType.DMA
    vmem = pltpu.VMEM
    any_spec = pl.BlockSpec(memory_space=pl.ANY)
    return pl.pallas_call(
        functools.partial(kernel, n_q, n_t, scale),
        out_shape=pltpu.VMEM((n_q, resident), F32),
        in_specs=[any_spec] * 5,
        out_specs=pl.BlockSpec(memory_space=pltpu.VMEM),
        scratch_shapes=[
            vmem((n_t, tokens, width), BF16),
            vmem((tokens, d_out), BF16),
            vmem((rank, d_out), BF16),
            vmem((n_t, resident, width), BF16),
            vmem((resident, d_out), BF16),
            vmem((n_t - 1, rank, width), BF16),
            vmem((n_t - 1, rank, width), BF16),
            vmem((n_t, n_q * rank, width), BF16),
            vmem((rank, d_out), BF16),
            vmem((n_t - 1, rank, d_out), BF16),
            vmem((n_q * rank, d_out), BF16),
            vmem((n_q * rank, resident), F32),
            dma((n_t + 2,)),
            dma(()), dma((n_t - 1,)),
            dma(()), dma((n_t - 1,)),
            dma(()), dma((n_chip - 1, n_t)), dma((n_t,)),
            dma(()), dma(()),
            dma(()), dma(()),
        ],
        compiler_params=pltpu.CompilerParams(
            collective_id=0, has_side_effects=True, vmem_limit_bytes=60 * 1024 * 1024
        ),
    )(query_acts[0], query_grads[0], sketch_maps[0], res_acts, res_grads)


def solution(mesh):
    in_specs = (
        P("query", "tok", None),
        P("query", "tok", None),
        P("query", None, None),
        P(("query", "tok"), None),
        P(("query", "tok"), None),
    )
    out_specs = P(None, ("query", "tok"))
    return jax.shard_map(local, mesh=mesh, in_specs=in_specs, out_specs=out_specs, check_vma=False)
```

```python
import functools
import math

import jax
import jax.numpy as jnp
from jax import lax
from jax.experimental import pallas as pl
from jax.experimental.pallas import tpu as pltpu
from jax.sharding import PartitionSpec as P

MESH = pl.DeviceIdType.MESH
F32 = jnp.float32
BF16 = jnp.bfloat16
HALVES = 2


def contract_last(first_arr, second_arr):
    return lax.dot_general(first_arr, second_arr, (((1,), (1,)), ((), ())), preferred_element_type=F32)


def spd_inverse(gram):
    size = gram.shape[0]
    rows = lax.broadcasted_iota(jnp.int32, (size, 2 * size), 0)
    cols = lax.broadcasted_iota(jnp.int32, (size, size), 1)
    eye = jnp.where(rows[:, :size] == cols, 1.0, 0.0).astype(F32)
    aug = jnp.concatenate([gram, eye], axis=1)
    for k in range(size):
        row = aug[k : k + 1, :] / aug[k : k + 1, k : k + 1]
        aug = jnp.where(rows == k, row, aug - aug[:, k : k + 1] * row)
    return aug[:, size:]


def kernel(
    n_q, n_t, scale,
    a_hbm, g_hbm, m_hbm, ra_hbm, rg_hbm, out_ref,
    a_buf, g_buf, m_buf, ra_buf, rg_buf,
    part_buf, rs_buf, s_all, r_mine, r_recv, x_all, acc,
    local_sem, rs_s, rs_r, z_s, z_r, s_s, c_r, b_r, f_s, f_r, x_s, x_r,
):
    q, z = lax.axis_index("query"), lax.axis_index("tok")
    n_chip = n_q // 2
    chip, core = q // 2, lax.rem(q, 2)
    sibling = chip * 2 + 1 - core
    rank = m_buf.shape[0]
    width = a_buf.shape[2]
    part_width = width // HALVES

    def tok_at(i):
        return lax.rem(z + i + n_t, n_t)

    def chip_at(c, which):
        return lax.rem(chip + c + n_chip, n_chip) * 2 + which

    barrier = pltpu.get_barrier_semaphore()
    for i in range(1, n_t):
        pl.semaphore_signal(barrier, inc=1, device_id=(q, tok_at(i)), device_id_type=MESH)
    for i in range(1, n_q):
        pl.semaphore_signal(barrier, inc=1, device_id=(lax.rem(q + i, n_q), z), device_id_type=MESH)

    def load(src, dst, sem):
        copy = pltpu.make_async_copy(src, dst, local_sem.at[sem])
        copy.start()
        return copy

    load_m = load(m_hbm, m_buf, 0)
    load_g = load(g_hbm, g_buf, 1)
    load_a, load_ra = [], []
    for i in range(n_t):
        t = tok_at(i + 1)
        load_a.append(load(a_hbm.at[:, pl.ds(pl.multiple_of(t * width, width), width)], a_buf.at[t], 2 + i))
    def remote(src, dst, send_sem, recv_sem, device):
        return pltpu.make_async_remote_copy(
            src_ref=src, dst_ref=dst, send_sem=send_sem, recv_sem=recv_sem, device_id=device, device_id_type=MESH
        )

    def send(src, dst, send_sem, recv_sem, device):
        remote(src, dst, send_sem, recv_sem, device).start()

    def landed(like, sem):
        remote(like, like, sem, sem, (sibling, z)).wait_recv()

    def left(like, sem):
        remote(like, like, sem, sem, (sibling, z)).wait_send()

    load_m.wait()
    load_g.wait()
    projected = contract_last(m_buf[...], g_buf[...]).astype(BF16)
    chunk = None
    for i in range(1, n_t + 1):
        t = tok_at(i)
        load_a[i - 1].wait()
        part = jnp.dot(projected, a_buf[t], preferred_element_type=F32)
        if i == n_t:
            chunk = part
        else:
            part_buf[i - 1] = part.astype(BF16)
    for i in range(n_t):
        t = tok_at(-i)
        load_ra.append(load(ra_hbm.at[:, pl.ds(pl.multiple_of(t * width, width), width)], ra_buf.at[t], 2 + i))
    load_rg = load(rg_hbm, rg_buf, 0)
    pl.semaphore_wait(barrier, n_t - 1 + n_q - 1)
    def columns(h):
        return pl.ds(h * part_width, part_width)

    for i in range(1, n_t):
        for h in range(HALVES):
            there = rs_buf.at[i - 1, :, columns(h)]
            send(part_buf.at[i - 1, :, columns(h)], there, rs_s, rs_r.at[i - 1, h], (q, tok_at(i)))

    def block(t, owner):
        return s_all.at[t, pl.ds(pl.multiple_of(owner * rank, rank), rank), :]

    def half_block(t, h):
        return s_all.at[t, pl.ds(pl.multiple_of(q * rank, rank), rank), columns(h)]

    def from_chip(c, i):
        return c_r.at[c - 1, i]

    def spread(i, h):
        here = half_block(tok_at(-i), h)
        for c in range(1, n_chip):
            send(here, here, s_s, from_chip(c, i), (chip_at(c, core), z))
        send(here, here, s_s, b_r.at[i], (sibling, z))

    def pull(i, h):
        t = tok_at(-i)
        return contract_last(half_block(t, h)[...], a_buf[t, :, columns(h)])

    def square(i):
        mine = s_all[tok_at(-i), pl.ds(pl.multiple_of(q * rank, rank), rank), :]
        return contract_last(mine, mine)

    pulled = jnp.zeros((rank, g_buf.shape[0]), F32)
    for h in range(HALVES):
        total = chunk[:, h * part_width : (h + 1) * part_width]
        for i in range(1, n_t):
            there = rs_buf.at[i - 1, :, columns(h)]
            landed(there, rs_r.at[i - 1, h])
            total = total + there[...].astype(F32)
        here = half_block(z, h)
        here[...] = total.astype(BF16)
        for i in range(1, n_t):
            send(here, here, z_s, z_r.at[i - 1, h], (q, tok_at(i)))
        spread(0, h)
        pulled += pull(0, h)
    gram = square(0)
    for h in range(HALVES):
        for i in range(1, n_t):
            landed(half_block(tok_at(-i), h), z_r.at[i - 1, h])
            spread(i, h)
            pulled += pull(i, h)
            if h == HALVES - 1 and i < n_t - 1:
                gram += square(i)
    high = pulled.astype(BF16)
    low = (pulled - high.astype(F32)).astype(BF16)
    grads = g_buf[...]
    right = jnp.dot(high, grads, preferred_element_type=F32) + jnp.dot(low, grads, preferred_element_type=F32)
    r_mine[...] = right.astype(BF16)
    for i in range(1, n_t):
        send(r_mine, r_recv.at[i - 1], f_s, f_r, (q, tok_at(i)))
    gram += square(n_t - 1)

    def relay(i):
        t = tok_at(-i)
        for c in range(1, n_chip):
            here = block(t, chip_at(-c, core))
            landed(here, from_chip(c, i))
            send(here, here, s_s, b_r.at[i], (sibling, z))

    def ready(i):
        landed(s_all.at[tok_at(-i), pl.ds(0, n_chip * rank)], b_r.at[i])
        load_ra[i].wait()

    def term(i):
        t = tok_at(-i)
        return contract_last(s_all[t], ra_buf[t])

    def score(i):
        ready(i)
        if i == 0:
            acc[...] = term(i)
        else:
            acc[...] += term(i)

    def x_block(owner):
        return x_all.at[pl.ds(pl.multiple_of(owner * rank, rank), rank), :]

    def solve(inverse, right):
        landed(r_recv, f_r)
        for i in range(1, n_t):
            right = right + r_recv[i - 1].astype(F32)
        solved = jnp.dot(inverse, right, precision=lax.Precision.HIGHEST, preferred_element_type=F32)
        x_all[pl.ds(pl.multiple_of(q * rank, rank), rank), :] = solved.astype(BF16)
        for i in (*range(2, n_q), 1):
            send(x_block(q), x_block(q), x_s, x_r, (lax.rem(q + i, n_q), z))

    relay(0)
    inverse = spd_inverse(gram)
    solve(inverse, right)
    relay(1)
    score(0)
    for i in range(2, n_t):
        relay(i)
        score(i - 1)
    ready(n_t - 1)
    last = tok_at(1 - n_t)
    acc[...] += contract_last(s_all[last, :, columns(0)], ra_buf[last, :, columns(0)])
    load_rg.wait()
    others = x_all.at[pl.ds(0, (n_q - 1) * rank), :]
    landed(others, x_r)
    product = contract_last(x_all[...], rg_buf[...]) * (acc[...] + contract_last(s_all[last, :, columns(1)], ra_buf[last, :, columns(1)]))
    totals = jnp.sum(product.reshape(n_q, rank, product.shape[1]), axis=1)
    out_ref[...] = totals * scale
    left(part_buf, rs_s)
    left(rs_buf, z_s)
    left(s_all.at[:, pl.ds(0, (n_q - 1) * rank), :], s_s)
    left(r_recv, f_s)
    left(others, x_s)


def local(query_acts, query_grads, sketch_maps, res_acts, res_grads):
    n_q, n_t = lax.axis_size("query"), lax.axis_size("tok")
    _, tokens, d_in = query_acts.shape
    d_out = query_grads.shape[2]
    rank = sketch_maps.shape[1]
    resident = res_acts.shape[0]
    width = d_in // n_t
    scale = 1.0 / math.sqrt(rank * d_out * tokens * n_t)
    n_chip = n_q // 2
    dma = pltpu.SemaphoreType.DMA
    vmem = pltpu.VMEM
    any_spec = pl.BlockSpec(memory_space=pl.ANY)
    return pl.pallas_call(
        functools.partial(kernel, n_q, n_t, scale),
        out_shape=pltpu.VMEM((n_q, resident), F32),
        in_specs=[any_spec] * 5,
        out_specs=pl.BlockSpec(memory_space=pltpu.VMEM),
        scratch_shapes=[
            vmem((n_t, tokens, width), BF16),
            vmem((tokens, d_out), BF16),
            vmem((rank, d_out), BF16),
            vmem((n_t, resident, width), BF16),
            vmem((resident, d_out), BF16),
            vmem((n_t - 1, rank, width), BF16),
            vmem((n_t - 1, rank, width), BF16),
            vmem((n_t, n_q * rank, width), BF16),
            vmem((rank, d_out), BF16),
            vmem((n_t - 1, rank, d_out), BF16),
            vmem((n_q * rank, d_out), BF16),
            vmem((n_q * rank, resident), F32),
            dma((n_t + 2,)),
            dma(()), dma((n_t - 1, HALVES)),
            dma(()), dma((n_t - 1, HALVES)),
            dma(()), dma((n_chip - 1, n_t)), dma((n_t,)),
            dma(()), dma(()),
            dma(()), dma(()),
        ],
        compiler_params=pltpu.CompilerParams(
            collective_id=0, has_side_effects=True, vmem_limit_bytes=60 * 1024 * 1024
        ),
    )(query_acts[0], query_grads[0], sketch_maps[0], res_acts, res_grads)


def solution(mesh):
    in_specs = (
        P("query", "tok", None),
        P("query", "tok", None),
        P("query", None, None),
        P(("query", "tok"), None),
        P(("query", "tok"), None),
    )
    out_specs = P(None, ("query", "tok"))
    return jax.shard_map(local, mesh=mesh, in_specs=in_specs, out_specs=out_specs, check_vma=False)
```

```python
import functools
import math

import jax
import jax.numpy as jnp
from jax import lax
from jax.experimental import pallas as pl
from jax.experimental.pallas import tpu as pltpu
from jax.sharding import PartitionSpec as P

MESH = pl.DeviceIdType.MESH
F32 = jnp.float32
BF16 = jnp.bfloat16
HALVES = 2


def contract_last(first_arr, second_arr):
    return lax.dot_general(first_arr, second_arr, (((1,), (1,)), ((), ())), preferred_element_type=F32)


def spd_inverse(gram):
    size = gram.shape[0]
    rows = lax.broadcasted_iota(jnp.int32, (size, 2 * size), 0)
    cols = lax.broadcasted_iota(jnp.int32, (size, size), 1)
    eye = jnp.where(rows[:, :size] == cols, 1.0, 0.0).astype(F32)
    aug = jnp.concatenate([gram, eye], axis=1)
    for k in range(size):
        row = aug[k : k + 1, :] / aug[k : k + 1, k : k + 1]
        aug = jnp.where(rows == k, row, aug - aug[:, k : k + 1] * row)
    return aug[:, size:]


def kernel(
    n_q, n_t, scale,
    a_hbm, g_hbm, m_hbm, ra_hbm, rg_hbm, out_ref,
    a_buf, g_buf, m_buf, ra_buf, rg_buf,
    part_buf, rs_buf, s_all, r_mine, r_recv, x_all, acc,
    local_sem, rs_s, rs_r, z_s, z_r, s_s, c_r, c_last, b_r, f_s, f_r, x_s, x_r,
):
    q, z = lax.axis_index("query"), lax.axis_index("tok")
    n_chip = n_q // 2
    chip, core = q // 2, lax.rem(q, 2)
    sibling = chip * 2 + 1 - core
    rank = m_buf.shape[0]
    width = a_buf.shape[2]
    part_width = width // HALVES

    def tok_at(i):
        return lax.rem(z + i + n_t, n_t)

    def chip_at(c, which):
        return lax.rem(chip + c + n_chip, n_chip) * 2 + which

    barrier = pltpu.get_barrier_semaphore()
    for i in range(1, n_t):
        pl.semaphore_signal(barrier, inc=1, device_id=(q, tok_at(i)), device_id_type=MESH)
    for i in range(1, n_q):
        pl.semaphore_signal(barrier, inc=1, device_id=(lax.rem(q + i, n_q), z), device_id_type=MESH)

    def load(src, dst, sem):
        copy = pltpu.make_async_copy(src, dst, local_sem.at[sem])
        copy.start()
        return copy

    load_m = load(m_hbm, m_buf, 0)
    load_g = load(g_hbm, g_buf, 1)
    load_a, load_ra = [], []
    for i in range(n_t):
        t = tok_at(i + 1)
        load_a.append(load(a_hbm.at[:, pl.ds(pl.multiple_of(t * width, width), width)], a_buf.at[t], 2 + i))
    def remote(src, dst, send_sem, recv_sem, device):
        return pltpu.make_async_remote_copy(
            src_ref=src, dst_ref=dst, send_sem=send_sem, recv_sem=recv_sem, device_id=device, device_id_type=MESH
        )

    def send(src, dst, send_sem, recv_sem, device):
        remote(src, dst, send_sem, recv_sem, device).start()

    def landed(like, sem):
        remote(like, like, sem, sem, (sibling, z)).wait_recv()

    def left(like, sem):
        remote(like, like, sem, sem, (sibling, z)).wait_send()

    load_m.wait()
    load_g.wait()
    projected = contract_last(m_buf[...], g_buf[...]).astype(BF16)
    chunk = None
    for i in range(1, n_t + 1):
        t = tok_at(i)
        load_a[i - 1].wait()
        part = jnp.dot(projected, a_buf[t], preferred_element_type=F32)
        if i == n_t:
            chunk = part
        else:
            part_buf[i - 1] = part.astype(BF16)
    for i in range(n_t):
        t = tok_at(-i)
        load_ra.append(load(ra_hbm.at[:, pl.ds(pl.multiple_of(t * width, width), width)], ra_buf.at[t], 2 + i))
    load_rg = load(rg_hbm, rg_buf, 0)
    pl.semaphore_wait(barrier, n_t - 1 + n_q - 1)
    def columns(h):
        return pl.ds(h * part_width, part_width)

    for i in range(1, n_t):
        for h in range(HALVES):
            there = rs_buf.at[i - 1, :, columns(h)]
            send(part_buf.at[i - 1, :, columns(h)], there, rs_s, rs_r.at[i - 1, h], (q, tok_at(i)))

    def block(t, owner):
        return s_all.at[t, pl.ds(pl.multiple_of(owner * rank, rank), rank), :]

    def half_block(t, h, owner=q):
        return s_all.at[t, pl.ds(pl.multiple_of(owner * rank, rank), rank), columns(h)]

    def from_chip(c, i, h):
        return c_last.at[c - 1] if (i, h) == (n_t - 1, HALVES - 1) else c_r.at[i, h if i else 0]

    def from_core(i, h):
        return b_r.at[i, h if i else 0]

    def spread(i, h):
        here = half_block(tok_at(-i), h)
        for c in range(1, n_chip):
            send(here, here, s_s, from_chip(c, i, h), (chip_at(c, core), z))
        send(here, here, s_s, from_core(i, h), (sibling, z))

    def pull(i, h):
        t = tok_at(-i)
        return contract_last(half_block(t, h)[...], a_buf[t, :, columns(h)])

    def square(i):
        mine = s_all[tok_at(-i), pl.ds(pl.multiple_of(q * rank, rank), rank), :]
        return contract_last(mine, mine)

    pulled = jnp.zeros((rank, g_buf.shape[0]), F32)
    for h in range(HALVES):
        total = chunk[:, h * part_width : (h + 1) * part_width]
        for i in range(1, n_t):
            there = rs_buf.at[i - 1, :, columns(h)]
            landed(there, rs_r.at[i - 1, h])
            total = total + there[...].astype(F32)
        here = half_block(z, h)
        here[...] = total.astype(BF16)
        for i in range(1, n_t):
            send(here, here, z_s, z_r.at[i - 1, h], (q, tok_at(i)))
        spread(0, h)
        pulled += pull(0, h)
    gram = square(0)
    for h in range(HALVES):
        for i in range(1, n_t):
            landed(half_block(tok_at(-i), h), z_r.at[i - 1, h])
            spread(i, h)
            pulled += pull(i, h)
            if h == HALVES - 1 and i < n_t - 1:
                gram += square(i)
    high = pulled.astype(BF16)
    low = (pulled - high.astype(F32)).astype(BF16)
    grads = g_buf[...]
    right = jnp.dot(high, grads, preferred_element_type=F32) + jnp.dot(low, grads, preferred_element_type=F32)
    r_mine[...] = right.astype(BF16)
    for i in range(1, n_t):
        send(r_mine, r_recv.at[i - 1], f_s, f_r, (q, tok_at(i)))
    gram += square(n_t - 1)

    def first(n, i, h):
        there = s_all.at[tok_at(-i), pl.ds(0, n * rank)]
        return there.at[:, columns(h)] if i else there

    def relay(i, h):
        t, chipwise = tok_at(-i), (i, h) == (n_t - 1, HALVES - 1)
        if not chipwise:
            landed(first(n_chip - 1, i, h), from_chip(1, i, h))
        for c in range(1, n_chip):
            owner = chip_at(-c, core)
            here = half_block(t, h, owner) if i else block(t, owner)
            if chipwise:
                landed(here, from_chip(c, i, h))
            send(here, here, s_s, from_core(i, h), (sibling, z))

    def ready(i, h):
        landed(first(n_chip, i, h), from_core(i, h))
        if h == 0:
            load_ra[i].wait()

    def term(i, h):
        t = tok_at(-i)
        return contract_last(s_all[t, :, columns(h)], ra_buf[t, :, columns(h)])

    def score(places, h):
        for i in places:
            ready(i, h)
        total = acc[...]
        for i in places:
            total = total + term(i, h)
        acc[...] = total

    def x_block(owner):
        return x_all.at[pl.ds(pl.multiple_of(owner * rank, rank), rank), :]

    def solve(inverse, right):
        landed(r_recv, f_r)
        for i in range(1, n_t):
            right = right + r_recv[i - 1].astype(F32)
        solved = jnp.dot(inverse, right, precision=lax.Precision.HIGHEST, preferred_element_type=F32)
        x_all[pl.ds(pl.multiple_of(q * rank, rank), rank), :] = solved.astype(BF16)
        for i in (*range(2, n_q), 1):
            send(x_block(q), x_block(q), x_s, x_r, (lax.rem(q + i, n_q), z))

    rest, final = range(1, n_t), HALVES - 1
    relay(0, 0)
    inverse = spd_inverse(gram)
    for i in rest[:-1]:
        relay(i, 0)
    solve(inverse, right)
    relay(n_t - 1, 0)
    ready(0, 0)
    acc[...] = contract_last(s_all[z], ra_buf[z])
    relay(1, final)
    score(rest, 0)
    for i in rest[1:-1]:
        relay(i, final)
    score(rest[:1], final)
    relay(n_t - 1, final)
    score(rest[1:-1], final)
    ready(n_t - 1, final)
    load_rg.wait()
    others = x_all.at[pl.ds(0, (n_q - 1) * rank), :]
    landed(others, x_r)
    product = contract_last(x_all[...], rg_buf[...]) * (acc[...] + term(n_t - 1, final))
    totals = jnp.sum(product.reshape(n_q, rank, product.shape[1]), axis=1)
    out_ref[...] = totals * scale
    left(part_buf, rs_s)
    left(rs_buf, z_s)
    left(s_all.at[:, pl.ds(0, (n_q - 1) * rank), :], s_s)
    left(r_recv, f_s)
    left(others, x_s)


def local(query_acts, query_grads, sketch_maps, res_acts, res_grads):
    n_q, n_t = lax.axis_size("query"), lax.axis_size("tok")
    _, tokens, d_in = query_acts.shape
    d_out = query_grads.shape[2]
    rank = sketch_maps.shape[1]
    resident = res_acts.shape[0]
    width = d_in // n_t
    scale = 1.0 / math.sqrt(rank * d_out * tokens * n_t)
    n_chip = n_q // 2
    dma = pltpu.SemaphoreType.DMA
    vmem = pltpu.VMEM
    any_spec = pl.BlockSpec(memory_space=pl.ANY)
    return pl.pallas_call(
        functools.partial(kernel, n_q, n_t, scale),
        out_shape=pltpu.VMEM((n_q, resident), F32),
        in_specs=[any_spec] * 5,
        out_specs=pl.BlockSpec(memory_space=pltpu.VMEM),
        scratch_shapes=[
            vmem((n_t, tokens, width), BF16),
            vmem((tokens, d_out), BF16),
            vmem((rank, d_out), BF16),
            vmem((n_t, resident, width), BF16),
            vmem((resident, d_out), BF16),
            vmem((n_t - 1, rank, width), BF16),
            vmem((n_t - 1, rank, width), BF16),
            vmem((n_t, n_q * rank, width), BF16),
            vmem((rank, d_out), BF16),
            vmem((n_t - 1, rank, d_out), BF16),
            vmem((n_q * rank, d_out), BF16),
            vmem((n_q * rank, resident), F32),
            dma((n_t + 2,)),
            dma(()), dma((n_t - 1, HALVES)),
            dma(()), dma((n_t - 1, HALVES)),
            dma(()), dma((n_t, HALVES)), dma((n_chip - 1,)), dma((n_t, HALVES)),
            dma(()), dma(()),
            dma(()), dma(()),
        ],
        compiler_params=pltpu.CompilerParams(
            collective_id=0, has_side_effects=True, vmem_limit_bytes=60 * 1024 * 1024
        ),
    )(query_acts[0], query_grads[0], sketch_maps[0], res_acts, res_grads)


def solution(mesh):
    in_specs = (
        P("query", "tok", None),
        P("query", "tok", None),
        P("query", None, None),
        P(("query", "tok"), None),
        P(("query", "tok"), None),
    )
    out_specs = P(None, ("query", "tok"))
    return jax.shard_map(local, mesh=mesh, in_specs=in_specs, out_specs=out_specs, check_vma=False)
```

```python
import functools
import math

import jax
import jax.numpy as jnp
from jax import lax
from jax.experimental import pallas as pl
from jax.experimental.pallas import tpu as pltpu
from jax.sharding import PartitionSpec as P

MESH = pl.DeviceIdType.MESH
F32 = jnp.float32
BF16 = jnp.bfloat16
HALVES = 2


def contract_last(first_arr, second_arr):
    return lax.dot_general(first_arr, second_arr, (((1,), (1,)), ((), ())), preferred_element_type=F32)


def spd_inverse(gram):
    size = gram.shape[0]
    rows = lax.broadcasted_iota(jnp.int32, (size, 2 * size), 0)
    cols = lax.broadcasted_iota(jnp.int32, (size, size), 1)
    eye = jnp.where(rows[:, :size] == cols, 1.0, 0.0).astype(F32)
    aug = jnp.concatenate([gram, eye], axis=1)
    for k in range(size):
        row = aug[k : k + 1, :] / aug[k : k + 1, k : k + 1]
        aug = jnp.where(rows == k, row, aug - aug[:, k : k + 1] * row)
    return aug[:, size:]


def kernel(
    n_q, n_t, scale,
    a_hbm, g_hbm, m_hbm, ra_hbm, rg_hbm, out_ref,
    a_buf, g_buf, m_buf, ra_buf, rg_buf,
    part_buf, rs_buf, s_all, r_mine, r_recv, x_all, acc,
    local_sem, rs_s, rs_r, z_s, z_r, s_s, c_r, c_last, b_r, f_s, f_r, x_s, x_r,
):
    q, z = lax.axis_index("query"), lax.axis_index("tok")
    n_chip = n_q // 2
    chip, core = q // 2, lax.rem(q, 2)
    sibling = chip * 2 + 1 - core
    rank = m_buf.shape[0]
    width = a_buf.shape[2]
    part_width = width // HALVES

    def tok_at(i):
        return lax.rem(z + i + n_t, n_t)

    def chip_at(c, which):
        return lax.rem(chip + c + n_chip, n_chip) * 2 + which

    barrier = pltpu.get_barrier_semaphore()
    for i in range(1, n_t):
        pl.semaphore_signal(barrier, inc=1, device_id=(q, tok_at(i)), device_id_type=MESH)
    for i in range(1, n_q):
        pl.semaphore_signal(barrier, inc=1, device_id=(lax.rem(q + i, n_q), z), device_id_type=MESH)

    def load(src, dst, sem):
        copy = pltpu.make_async_copy(src, dst, local_sem.at[sem])
        copy.start()
        return copy

    load_m = load(m_hbm, m_buf, 0)
    load_g = load(g_hbm, g_buf, 1)
    load_a, load_ra = [], []
    for i in range(n_t):
        t = tok_at(i + 1)
        load_a.append(load(a_hbm.at[:, pl.ds(pl.multiple_of(t * width, width), width)], a_buf.at[t], 2 + i))
    def remote(src, dst, send_sem, recv_sem, device):
        return pltpu.make_async_remote_copy(
            src_ref=src, dst_ref=dst, send_sem=send_sem, recv_sem=recv_sem, device_id=device, device_id_type=MESH
        )

    def send(src, dst, send_sem, recv_sem, device):
        remote(src, dst, send_sem, recv_sem, device).start()

    def landed(like, sem):
        remote(like, like, sem, sem, (sibling, z)).wait_recv()

    def left(like, sem):
        remote(like, like, sem, sem, (sibling, z)).wait_send()

    load_m.wait()
    load_g.wait()
    projected = contract_last(m_buf[...], g_buf[...]).astype(BF16)
    chunk = None
    for i in range(1, n_t + 1):
        t = tok_at(i)
        load_a[i - 1].wait()
        part = jnp.dot(projected, a_buf[t], preferred_element_type=F32)
        if i == n_t:
            chunk = part
        else:
            part_buf[i - 1] = part.astype(BF16)
    for i in range(n_t):
        t = tok_at(-i)
        load_ra.append(load(ra_hbm.at[:, pl.ds(pl.multiple_of(t * width, width), width)], ra_buf.at[t], 2 + i))
    load_rg = load(rg_hbm, rg_buf, 0)
    pl.semaphore_wait(barrier, n_t - 1 + n_q - 1)
    def columns(h):
        return pl.ds(h * part_width, part_width)

    for i in range(1, n_t):
        for h in range(HALVES):
            there = rs_buf.at[i - 1, :, columns(h)]
            send(part_buf.at[i - 1, :, columns(h)], there, rs_s, rs_r.at[i - 1, h], (q, tok_at(i)))

    def block(t, owner):
        return s_all.at[t, pl.ds(pl.multiple_of(owner * rank, rank), rank), :]

    def half_block(t, h, owner=q):
        return s_all.at[t, pl.ds(pl.multiple_of(owner * rank, rank), rank), columns(h)]

    def slot(i, h):
        return (i - 1) * HALVES + h + 1 if i else 0

    def from_chip(c, i, h):
        return c_last.at[c - 1] if (i, h) == (n_t - 1, HALVES - 1) else c_r.at[slot(i, h)]

    def from_core(i, h):
        return b_r.at[slot(i, h)]

    def spread(i, h):
        here = half_block(tok_at(-i), h)
        for c in range(1, n_chip):
            send(here, here, s_s, from_chip(c, i, h), (chip_at(c, core), z))
        send(here, here, s_s, from_core(i, h), (sibling, z))

    def pull(i, h):
        t = tok_at(-i)
        return contract_last(half_block(t, h)[...], a_buf[t, :, columns(h)])

    def square(i):
        mine = s_all[tok_at(-i), pl.ds(pl.multiple_of(q * rank, rank), rank), :]
        return contract_last(mine, mine)

    pulled = jnp.zeros((rank, g_buf.shape[0]), F32)
    for h in range(HALVES):
        total = chunk[:, h * part_width : (h + 1) * part_width]
        for i in range(1, n_t):
            there = rs_buf.at[i - 1, :, columns(h)]
            landed(there, rs_r.at[i - 1, h])
            total = total + there[...].astype(F32)
        here = half_block(z, h)
        here[...] = total.astype(BF16)
        for i in range(1, n_t):
            send(here, here, z_s, z_r.at[i - 1, h], (q, tok_at(i)))
        spread(0, h)
        pulled += pull(0, h)
    gram = square(0)
    for h in range(HALVES):
        for i in range(1, n_t):
            landed(half_block(tok_at(-i), h), z_r.at[i - 1, h])
            spread(i, h)
            pulled += pull(i, h)
            if h == HALVES - 1 and i < n_t - 1:
                gram += square(i)
    high = pulled.astype(BF16)
    low = (pulled - high.astype(F32)).astype(BF16)
    grads = g_buf[...]
    right = jnp.dot(high, grads, preferred_element_type=F32) + jnp.dot(low, grads, preferred_element_type=F32)
    r_mine[...] = right.astype(BF16)
    for i in range(1, n_t):
        send(r_mine, r_recv.at[i - 1], f_s, f_r, (q, tok_at(i)))
    gram += square(n_t - 1)

    def first(n, i, h):
        there = s_all.at[tok_at(-i), pl.ds(0, n * rank)]
        return there.at[:, columns(h)] if i else there

    def relay(i, h):
        t, chipwise = tok_at(-i), (i, h) == (n_t - 1, HALVES - 1)
        if not chipwise:
            landed(first(n_chip - 1, i, h), from_chip(1, i, h))
        for c in range(1, n_chip):
            owner = chip_at(-c, core)
            here = half_block(t, h, owner) if i else block(t, owner)
            if chipwise:
                landed(here, from_chip(c, i, h))
            send(here, here, s_s, from_core(i, h), (sibling, z))

    def ready(i, h):
        landed(first(n_chip, i, h), from_core(i, h))
        if h == 0:
            load_ra[i].wait()

    def term(i, h):
        t = tok_at(-i)
        return contract_last(s_all[t, :, columns(h)], ra_buf[t, :, columns(h)])

    def score(places, h):
        for i in places:
            ready(i, h)
        total = acc[...]
        for i in places:
            total = total + term(i, h)
        acc[...] = total

    def x_block(owner):
        return x_all.at[pl.ds(pl.multiple_of(owner * rank, rank), rank), :]

    def solve(inverse, right):
        landed(r_recv, f_r)
        for i in range(1, n_t):
            right = right + r_recv[i - 1].astype(F32)
        solved = jnp.dot(inverse, right, precision=lax.Precision.HIGHEST, preferred_element_type=F32)
        x_all[pl.ds(pl.multiple_of(q * rank, rank), rank), :] = solved.astype(BF16)
        for i in (*range(2, n_q), 1):
            send(x_block(q), x_block(q), x_s, x_r, (lax.rem(q + i, n_q), z))

    rest, final = range(1, n_t), HALVES - 1
    relay(0, 0)
    inverse = spd_inverse(gram)
    for i in rest[:-1]:
        relay(i, 0)
    solve(inverse, right)
    relay(n_t - 1, 0)
    ready(0, 0)
    acc[...] = contract_last(s_all[z], ra_buf[z])
    relay(1, final)
    score(rest, 0)
    for i in rest[1:-1]:
        relay(i, final)
    score(rest[:1], final)
    relay(n_t - 1, final)
    score(rest[1:-1], final)
    ready(n_t - 1, final)
    load_rg.wait()
    others = x_all.at[pl.ds(0, (n_q - 1) * rank), :]
    landed(others, x_r)
    product = contract_last(x_all[...], rg_buf[...]) * (acc[...] + term(n_t - 1, final))
    totals = jnp.sum(product.reshape(n_q, rank, product.shape[1]), axis=1)
    out_ref[...] = totals * scale
    left(part_buf, rs_s)
    left(rs_buf, z_s)
    left(s_all.at[:, pl.ds(0, (n_q - 1) * rank), :], s_s)
    left(r_recv, f_s)
    left(others, x_s)


def local(query_acts, query_grads, sketch_maps, res_acts, res_grads):
    n_q, n_t = lax.axis_size("query"), lax.axis_size("tok")
    _, tokens, d_in = query_acts.shape
    d_out = query_grads.shape[2]
    rank = sketch_maps.shape[1]
    resident = res_acts.shape[0]
    width = d_in // n_t
    scale = 1.0 / math.sqrt(rank * d_out * tokens * n_t)
    n_chip = n_q // 2
    dma = pltpu.SemaphoreType.DMA
    vmem = pltpu.VMEM
    any_spec = pl.BlockSpec(memory_space=pl.ANY)
    return pl.pallas_call(
        functools.partial(kernel, n_q, n_t, scale),
        out_shape=pltpu.VMEM((n_q, resident), F32),
        in_specs=[any_spec] * 5,
        out_specs=pl.BlockSpec(memory_space=pltpu.VMEM),
        scratch_shapes=[
            vmem((n_t, tokens, width), BF16),
            vmem((tokens, d_out), BF16),
            vmem((rank, d_out), BF16),
            vmem((n_t, resident, width), BF16),
            vmem((resident, d_out), BF16),
            vmem((n_t - 1, rank, width), BF16),
            vmem((n_t - 1, rank, width), BF16),
            vmem((n_t, n_q * rank, width), BF16),
            vmem((rank, d_out), BF16),
            vmem((n_t - 1, rank, d_out), BF16),
            vmem((n_q * rank, d_out), BF16),
            vmem((n_q * rank, resident), F32),
            dma((n_t + 2,)),
            dma(()), dma((n_t - 1, HALVES)),
            dma(()), dma((n_t - 1, HALVES)),
            dma(()), dma(((n_t - 1) * HALVES,)), dma((n_chip - 1,)), dma(((n_t - 1) * HALVES + 1,)),
            dma(()), dma(()),
            dma(()), dma(()),
        ],
        compiler_params=pltpu.CompilerParams(
            collective_id=0, has_side_effects=True, vmem_limit_bytes=60 * 1024 * 1024
        ),
    )(query_acts[0], query_grads[0], sketch_maps[0], res_acts, res_grads)


def solution(mesh):
    in_specs = (
        P("query", "tok", None),
        P("query", "tok", None),
        P("query", None, None),
        P(("query", "tok"), None),
        P(("query", "tok"), None),
    )
    out_specs = P(None, ("query", "tok"))
    return jax.shard_map(local, mesh=mesh, in_specs=in_specs, out_specs=out_specs, check_vma=False)
```
